32 devices in a mesh: groups: 2 (over x), frame: 16 (over z, y, core).
Axes of the slice: x: 2, y: 2, z: 4, core: 2. Of those that a mesh axis runs over, the one named last changes fastest.
Arguments:
- queries: bfloat16 [4096, 2048], P(('groups', 'frame')), parts along dimension 0, may hold values from -40 to 40, as said below
- key_rows: bfloat16 [4096, 2048], P(('groups', 'frame')), parts along dimension 0, may hold values from -4 to 4
- value_rows: bfloat16 [4096, 2048], P(('groups', 'frame')), parts along dimension 0, may hold values from -6 to 6
- slopes: bfloat16 [16], replicated, may hold values from 0.0019989014 to 0.19921875
- noise_level: int32 [32], P('groups'), parts along dimension 0, may hold values from 0 to 999
- frame_times: int32 [32], P('groups'), parts along dimension 0, may hold values from 0 to 30, as said below
Outputs:
- advanced: bfloat16 [4096, 2048], P(('groups', 'frame')), parts along dimension 0
The draws below stay inside these ranges and needn't reach their ends.
There are 2 independent parts, one for each index of `groups`. The reference program is written for one: setup_inputs(seed, part) draws one part's arguments, and reference() takes and returns one part's arrays. A program takes and returns all parts, laid end to end along the dimension named above; an argument that names none is the same for every part. Nothing has to cross between parts.
Inputs may be any that keep to these rules, and one draw needn't show every extreme that they name: Rows of queries may be large multiples of key rows. `frame_times`: strictly increasing along the window, starting at 0; neighbouring frames differ by 1 to 3; the last frame stands at 30.
All inputs are finite; a program needn't handle non-finite values.
Results may differ from the reference program's by a relative error of at most 0.009.
Values may be sent and summed in bfloat16 or wider, within the bound.
No kernel may reach another device: no remote copies, remote signals or barrier semaphores. Data moves between devices by JAX's collectives and lax.ppermute only.
A program may use at most 64 MiB of HBM per device.

```python
import math
import jax
import jax.numpy as jnp
from jax import lax

H = 16
HD = 128
D = 2048
FT = 128
FRAMES = 16
TOKENS = 2048
LEVELS = 1000


def paired_rows(key):
    base = jax.random.fold_in(key, 7)
    query_key, row_key = jax.random.split(base, 2)
    total = FRAMES * FT
    query_vals = jnp.clip(jax.random.normal(query_key, (total, D), jnp.float32), -4.0, 4.0)
    key_vals = jnp.clip(jax.random.normal(row_key, (total, D), jnp.float32), -4.0, 4.0)
    return (query_vals, key_vals)


def draw_queries(key, part):
    return paired_rows(key)[0].astype(jnp.bfloat16)


def draw_key_rows(key, part):
    return paired_rows(key)[1].astype(jnp.bfloat16)


def draw_frame_times(key, part):
    gap_count = FRAMES - 1
    half_count = (FRAMES - 2) // 2
    position = jnp.arange(gap_count, dtype=jnp.int32)
    offsets = jnp.where(position < half_count, -1, jnp.where(position < 2 * half_count, 1, 0)).astype(jnp.int32)
    mixed_offsets = jax.random.permutation(jax.random.fold_in(key, 11), offsets)
    gaps = 2 + mixed_offsets
    stamps = jnp.concatenate([jnp.zeros((1,), jnp.int32), jnp.cumsum(gaps).astype(jnp.int32)])
    return stamps.astype(jnp.int32)


def place_ends(array, own_key, low, high):
    longest = array.shape.index(max(array.shape))
    spots = []
    for shift in (0, 1):
        where = [jax.random.randint(jax.random.fold_in(own_key, axis), (), 0, length) for axis, length in enumerate(array.shape)]
        where[longest] = (where[longest] + shift) % array.shape[longest]
        spots.append(tuple(where))
    return array.at[spots[0]].set(low).at[spots[1]].set(high)


def shard_levels(rng, extent, cuts, least, largest):
    def one(dim, shards_of):
        steps = jax.random.uniform(jax.random.fold_in(jax.random.fold_in(rng, 6), dim), (shards_of,), jnp.float32, least / len(cuts), largest / len(cuts))
        return jnp.repeat(jnp.exp(steps), extent[dim] // shards_of).reshape((-1,) + (1,) * (len(extent) - dim - 1))

    factor_of = one(*cuts[0])
    for cut in cuts[1:]:
        factor_of = factor_of * one(*cut)
    return factor_of


def normal_values(stream_key, extent, width, limit, shards=(), held_as=jnp.bfloat16):
    drawn = width * jax.random.normal(stream_key, extent, jnp.float32)
    if shards:
        drawn = drawn * shard_levels(stream_key, extent, shards, -0.22, 0.18)
    return jnp.clip(drawn, -limit, limit).astype(held_as)


def setup_inputs(seed: int = 0, part: int = 0) -> dict:
    seeds = jax.random.split(jax.random.key(seed), 7)
    part_keys = jax.random.split(jax.random.fold_in(seeds[6], part), 7)
    return {
        "queries": draw_queries(jax.random.fold_in(jax.random.fold_in(seeds[6], part), 71), part),
        "key_rows": draw_key_rows(jax.random.fold_in(jax.random.fold_in(seeds[6], part), 71), part),
        "value_rows": normal_values(part_keys[2], (TOKENS, D), 1.0, 6.0, ((0, 16),)),
        "slopes": jnp.clip(jnp.exp(jax.random.uniform(seeds[3], (H,), jnp.float32, math.log(0.0019989014), math.log(0.19921875))), 0.0019989014, 0.19921875).astype(jnp.bfloat16),
        "noise_level": place_ends(jax.random.randint(part_keys[4], (FRAMES,), 0, LEVELS), jax.random.fold_in(part_keys[4], 1), 0, LEVELS - 1).astype(jnp.int32),
        "frame_times": draw_frame_times(jax.random.fold_in(jax.random.fold_in(seeds[6], part), 71), part),
    }


def noise_gates(noise_level):
    phase = (noise_level.astype(jnp.float32) / LEVELS + 0.008) / 1.008
    cosine = jnp.cos(phase * (math.pi / 2))
    signal = cosine * cosine
    return (jnp.sqrt(signal), jnp.sqrt(1.0 - signal))

def spatial_frame(block):
    query_frame, key_frame, value_frame = block
    query_heads = query_frame.reshape(FT, H, HD).astype(jnp.float32)
    key_heads = key_frame.reshape(FT, H, HD).astype(jnp.float32)
    value_heads = value_frame.reshape(FT, H, HD).astype(jnp.float32)
    scores = jnp.einsum('qhd,khd->hqk', query_heads, key_heads) / math.sqrt(HD)
    weights = jax.nn.softmax(scores, axis=-1).astype(jnp.bfloat16)
    attended = jnp.einsum('hqk,khd->qhd', weights.astype(jnp.float32), value_heads)
    return attended.reshape(FT, H * HD)

def reference(queries, key_rows, value_rows, slopes, noise_level, frame_times):
    signal_gate, noise_gate = noise_gates(noise_level)
    framed = (queries.reshape(FRAMES, FT, D), key_rows.reshape(FRAMES, FT, D), value_rows.reshape(FRAMES, FT, D))
    spatial = lax.map(spatial_frame, framed)
    distance = jnp.abs(frame_times[:, None] - frame_times[None, :]).astype(jnp.float32)
    penalty = -slopes.astype(jnp.float32)[:, None, None] * distance[None]
    blk_size = math.gcd(FT, 64)
    blk_count = FT // blk_size

    def arrange(source):
        return jnp.moveaxis(source.reshape(FRAMES, blk_count, blk_size, H, HD), 1, 0)

    def temporal_block(block):
        query_blk, key_blk, value_blk = block
        scores = jnp.einsum('qbhd,kbhd->bhqk', query_blk.astype(jnp.float32), key_blk.astype(jnp.float32)) / math.sqrt(HD)
        scores = scores + penalty[None]
        weights = jax.nn.softmax(scores, axis=-1).astype(jnp.bfloat16)
        attended = jnp.einsum('bhqk,kbhd->qbhd', weights.astype(jnp.float32), value_blk.astype(jnp.float32))
        return (attended * noise_gate[:, None, None, None]).astype(jnp.bfloat16)
    temporal = lax.map(temporal_block, (arrange(queries), arrange(key_rows), arrange(value_rows)))
    temporal = jnp.moveaxis(temporal, 0, 1).reshape(FRAMES, FT, D)
    mixed = (signal_gate[:, None, None] * spatial + temporal.astype(jnp.float32)).astype(jnp.bfloat16)
    mixed = mixed.reshape(TOKENS, D)
    return jnp.concatenate([mixed[FT:], jnp.zeros((FT, D), jnp.bfloat16)], axis=0)
```

```python
import functools
import math

import jax
import jax.numpy as jnp
from jax import lax
from jax.experimental import pallas as pl
from jax.experimental.pallas import tpu as pltpu
from jax.sharding import PartitionSpec as P

LEVELS = 1000
FAR = 1e30
VMEM_BYTES = 24 << 20


def shifted(value, axis, steps):
    count = lax.axis_size(axis)
    first, last = (max(0, -steps), min(count, count - steps))
    return lax.ppermute(value, axis, [(source, source + steps) for source in range(first, last)])


def noise_gates(noise_level):
    phase = (noise_level.astype(jnp.float32) / LEVELS + 0.008) / 1.008
    cosine = jnp.cos(phase * (math.pi / 2))
    signal = cosine * cosine
    return (jnp.sqrt(signal), jnp.sqrt(1.0 - signal))


def head_attention(query, key, value, scale, penalty):
    scores = lax.dot_general(query, key, (((1,), (1,)), ((), ())), preferred_element_type=jnp.float32) * scale
    if penalty is not None:
        scores = scores - penalty
    peak = jnp.max(scores, axis=-1, keepdims=True)
    raised = jnp.exp(scores - peak)
    weights = (raised * (1.0 / jnp.sum(raised, axis=-1, keepdims=True))).astype(jnp.bfloat16)
    return jnp.dot(weights, value, preferred_element_type=jnp.float32)


def temporal_kernel(head_dim, share, slopes_ref, moved_ref, distance_ref, gate_ref, out_ref):
    rows, width = out_ref.shape
    distance = distance_ref[...]
    gate = gate_ref[...]
    kept = lax.broadcasted_iota(jnp.int32, (rows, head_dim), 0) < rows - share
    for head in range(width // head_dim):
        spans = [pl.ds(part * width + head * head_dim, head_dim) for part in range(3)]
        attended = head_attention(
            moved_ref[:, spans[0]],
            moved_ref[:, spans[1]],
            moved_ref[:, spans[2]],
            1.0 / math.sqrt(head_dim),
            slopes_ref[head] * distance,
        )
        earlier = pltpu.roll(attended * gate, rows - share, 0)
        out_ref[:, spans[0]] = jnp.where(kept, earlier, 0.0).astype(out_ref.dtype)


def spatial_kernel(head_dim, gate_ref, query_ref, key_ref, value_ref, out_ref):
    rows, width = out_ref.shape
    gate = gate_ref[0]
    for head in range(width // head_dim):
        span = pl.ds(head * head_dim, head_dim)
        attended = head_attention(
            query_ref[:, span], key_ref[:, span], value_ref[:, span], 1.0 / math.sqrt(head_dim), None
        )
        out_ref[:, span] = (attended * gate).astype(out_ref.dtype)


def cost(rows, width, operands):
    return pl.CostEstimate(
        flops=4 * rows * rows * width, bytes_accessed=operands * 2 * rows * width, transcendentals=rows * rows * 16
    )


def body(queries, key_rows, value_rows, slopes, noise_level, frame_times):
    frame_rows, model_width = queries.shape
    head_count = slopes.shape[0]
    head_dim = model_width // head_count
    count = lax.axis_size("frame")
    share = frame_rows // count
    vmem = pl.BlockSpec(memory_space=pltpu.VMEM)
    smem = pl.BlockSpec(memory_space=pltpu.SMEM)
    signal_gate, noise_gate = noise_gates(noise_level)
    own_gate = lax.dynamic_slice_in_dim(signal_gate, lax.axis_index("frame"), 1)

    moved = lax.all_to_all(
        jnp.concatenate([queries, key_rows, value_rows], axis=1), "frame", split_axis=0, concat_axis=0, tiled=True
    )

    spatial = pl.pallas_call(
        functools.partial(spatial_kernel, head_dim),
        out_shape=jax.ShapeDtypeStruct((frame_rows, model_width), jnp.bfloat16),
        in_specs=[smem, vmem, vmem, vmem],
        out_specs=vmem,
        cost_estimate=cost(frame_rows, model_width, 4),
        compiler_params=pltpu.CompilerParams(vmem_limit_bytes=VMEM_BYTES),
        name="spatial",
    )(own_gate, queries, key_rows, value_rows)
    carried = shifted(spatial, "frame", -1)

    rows = count * share
    row_times = jnp.repeat(frame_times.astype(jnp.float32), share)
    row_tokens = lax.rem(jnp.arange(rows), share)
    distance = jnp.where(
        row_tokens[:, None] == row_tokens[None, :], jnp.abs(row_times[:, None] - row_times[None, :]), FAR
    )
    gate_rows = jnp.broadcast_to(jnp.repeat(noise_gate, share)[:, None], (rows, head_dim))
    temporal = pl.pallas_call(
        functools.partial(temporal_kernel, head_dim, share),
        out_shape=jax.ShapeDtypeStruct((rows, model_width), jnp.bfloat16),
        in_specs=[smem, vmem, vmem, vmem],
        out_specs=vmem,
        cost_estimate=cost(rows, model_width, 4),
        compiler_params=pltpu.CompilerParams(vmem_limit_bytes=VMEM_BYTES),
        name="temporal",
    )(slopes.astype(jnp.float32), moved, distance, gate_rows)
    returned = lax.all_to_all(temporal, "frame", split_axis=0, concat_axis=0, tiled=True)
    return (carried.astype(jnp.float32) + returned.astype(jnp.float32)).astype(jnp.bfloat16)


def solution(mesh):
    return jax.shard_map(
        body,
        mesh=mesh,
        in_specs=(
            P(("groups", "frame"), None),
            P(("groups", "frame"), None),
            P(("groups", "frame"), None),
            P(),
            P("groups"),
            P("groups"),
        ),
        out_specs=P(("groups", "frame"), None),
        check_vma=False,
    )
```

```python
import functools
import math

import jax
import jax.numpy as jnp
from jax import lax
from jax.experimental import pallas as pl
from jax.experimental.pallas import tpu as pltpu
from jax.sharding import PartitionSpec as P


LEVELS = 1000
FAR = 1e30
VMEM_BYTES = 24 << 20
SUBLANES = 8
EARLY = 2
LOG2_E = math.log2(math.e)
VMEM = pl.BlockSpec(memory_space=pltpu.VMEM)
SMEM = pl.BlockSpec(memory_space=pltpu.SMEM)
HBM = pl.BlockSpec(memory_space=pltpu.HBM)
ANY = pl.BlockSpec(memory_space=pl.ANY)


def shifted(value, axis, steps):
    count = lax.axis_size(axis)
    first, last = (max(0, -steps), min(count, count - steps))
    return lax.ppermute(value, axis, [(source, source + steps) for source in range(first, last)])


def paired(value, step):
    count = lax.axis_size("frame")
    return lax.ppermute(value, "frame", [(device, device ^ step) for device in range(count)])


def noise_gates(noise_level):
    phase = (noise_level.astype(jnp.float32) / LEVELS + 0.008) / 1.008
    cosine = jnp.cos(phase * (math.pi / 2))
    signal = cosine * cosine
    return (jnp.sqrt(signal), jnp.sqrt(1.0 - signal))


def in_pairs(frame_rows, count):
    return frame_rows % (SUBLANES * count) == 0 and count >= 4 and count & (count - 1) == 0


def far_steps(count):
    half, quarter = count // 2, count // 4
    return [half + offset + side for offset in range(quarter) for side in (quarter, 0)]


def near_steps(count):
    return list(range(count // 2 - 1, 0, -1))


def attend_heads(query_of, key_of, value_of, slope_of, distance, head_count, head_dim):
    factor = LOG2_E / math.sqrt(head_dim)
    heads = range(head_count)
    scores = [
        lax.dot_general(key_of(head), query_of(head), (((1,), (1,)), ((), ())), preferred_element_type=jnp.float32)
        * factor
        for head in heads
    ]
    if distance is not None:
        scores = [score - (slope_of(head) * LOG2_E) * distance for score, head in zip(scores, heads)]
    peaks = [jnp.max(score, axis=0, keepdims=True) for score in scores]
    raised = [jnp.exp2(score - peak) for score, peak in zip(scores, peaks)]
    shares = [1.0 / jnp.sum(value, axis=0, keepdims=True) for value in raised]
    weights = [(value * share).astype(jnp.bfloat16) for value, share in zip(raised, shares)]
    return [
        lax.dot_general(weight, value_of(head), (((0,), (0,)), ((), ())), preferred_element_type=jnp.float32)
        for weight, head in zip(weights, heads)
    ]


def run_copies(sem, pairs):
    copies = [pltpu.make_async_copy(source, target, sem.at[place]) for place, (source, target) in enumerate(pairs)]
    for copy in copies:
        copy.start()
    for copy in copies:
        copy.wait()


def rows_at(ref, block, share):
    return ref.at[pl.ds(pl.multiple_of(block * share, share), share), :]


def gather_kernel(steps, share, width, query_ref, key_ref, value_ref, *rest):
    outs, sem = rest[:-1], rest[-1]
    me = lax.axis_index("frame")
    pairs = []
    for place, step in enumerate(steps):
        start = pl.multiple_of((me ^ step) * share, share)
        for part, source in enumerate((query_ref, key_ref, value_ref)):
            pairs.append(
                (source.at[pl.ds(start, share), pl.ds(0, width)], outs[place].at[:, pl.ds(part * width, width)])
            )
    run_copies(sem, pairs)


def paired_kernel(count, head_dim, share, slopes_ref, distance_ref, gate_ref, *rest):
    blocks, out_ref, moved_ref, result_ref, sem = rest[:count], *rest[count:]
    width = result_ref.shape[1]
    gate = gate_ref[...]
    for step, block in enumerate(blocks):
        moved_ref[pl.ds(step * share, share), :] = block[...]
    part = lambda index: lambda head: moved_ref[:, pl.ds(index * width + head * head_dim, head_dim)]
    attended = attend_heads(
        part(0), part(1), part(2), lambda head: slopes_ref[head], distance_ref[...], width // head_dim, head_dim
    )
    for head, value in enumerate(attended):
        result_ref[:, pl.ds(head * head_dim, head_dim)] = (value * gate).astype(result_ref.dtype)
    me = lax.axis_index("frame")
    pairs = []
    for step in range(count):
        slot = lax.rem((me ^ step) + count - 1, count)
        pairs.append((result_ref.at[pl.ds(step * share, share), :], rows_at(out_ref, slot, share)))
    run_copies(sem, pairs)


def plain_kernel(head_dim, share, slopes_ref, distance_ref, gate_ref, moved_ref, out_ref):
    rows, width = out_ref.shape
    gate = gate_ref[...]
    kept = lax.broadcasted_iota(jnp.int32, (rows, head_dim), 0) < rows - share
    part = lambda index: lambda head: moved_ref[:, pl.ds(index * width + head * head_dim, head_dim)]
    attended = attend_heads(
        part(0), part(1), part(2), lambda head: slopes_ref[head], distance_ref[...], width // head_dim, head_dim
    )
    for head, value in enumerate(attended):
        earlier = pltpu.roll(value * gate, rows - share, 0)
        out_ref[:, pl.ds(head * head_dim, head_dim)] = jnp.where(kept, earlier, 0.0).astype(out_ref.dtype)


def spatial_kernel(head_dim, gate_ref, query_ref, key_ref, value_ref, out_ref):
    width = out_ref.shape[1]
    gate = gate_ref[lax.axis_index("frame")]
    part = lambda ref: lambda head: ref[:, pl.ds(head * head_dim, head_dim)]
    attended = attend_heads(part(query_ref), part(key_ref), part(value_ref), None, None, width // head_dim, head_dim)
    for head, value in enumerate(attended):
        out_ref[:, pl.ds(head * head_dim, head_dim)] = (value * gate).astype(out_ref.dtype)


def cost(rows, width, operands):
    return pl.CostEstimate(
        flops=4 * rows * rows * width, bytes_accessed=operands * 2 * rows * width, transcendentals=rows * rows * 16
    )


def params():
    return pltpu.CompilerParams(vmem_limit_bytes=VMEM_BYTES)


def table_kernel(crossed, share, times_ref, gate_ref, distance_ref, rows_ref):
    rows, width = distance_ref.shape[0], rows_ref.shape[1]
    count = rows // share
    me = lax.axis_index("frame")
    owners = [me ^ place if crossed else place for place in range(count)]
    times = [times_ref[owner].astype(jnp.float32) for owner in owners]
    lane = lax.broadcasted_iota(jnp.int32, (share, rows), 1)
    row = lax.broadcasted_iota(jnp.int32, (share, rows), 0)
    lane_times = jnp.zeros((share, rows), jnp.float32)
    for place, time in enumerate(times):
        lane_times = jnp.where(lax.div(lane, share) == place, time, lane_times)
    same = lax.rem(lane, share) == row
    for place, (owner, time) in enumerate(zip(owners, times)):
        span = pl.ds(place * share, share)
        distance_ref[span, :] = jnp.where(same, jnp.abs(lane_times - time), FAR)
        gate = jnp.where(owner > 0, gate_ref[owner], 0.0)
        rows_ref[span, :] = jnp.full((share, width), gate, jnp.float32)


def tables(frame_times, noise_gate, crossed, share, head_dim):
    rows = frame_times.shape[0] * share
    return pl.pallas_call(
        functools.partial(table_kernel, crossed, share),
        out_shape=[
            jax.ShapeDtypeStruct((rows, rows), jnp.float32),
            jax.ShapeDtypeStruct((rows, head_dim), jnp.float32),
        ],
        in_specs=[SMEM, SMEM],
        out_specs=[VMEM, VMEM],
        compiler_params=params(),
        name="tables",
    )(frame_times, noise_gate)


def spatial_part(queries, key_rows, value_rows, signal_gate, head_dim):
    frame_rows, model_width = queries.shape
    spatial = pl.pallas_call(
        functools.partial(spatial_kernel, head_dim),
        out_shape=jax.ShapeDtypeStruct((frame_rows, model_width), jnp.bfloat16),
        in_specs=[SMEM, VMEM, VMEM, VMEM],
        out_specs=VMEM,
        cost_estimate=cost(frame_rows, model_width, 4),
        compiler_params=params(),
        name="spatial",
    )(signal_gate, queries, key_rows, value_rows)
    return shifted(spatial, "frame", -1)


def exchanged(arrays, slopes, distance, gate_rows, head_dim, share):
    rows, width = arrays[0].shape
    moved = lax.all_to_all(jnp.concatenate(arrays, axis=1), "frame", split_axis=0, concat_axis=0, tiled=True)
    temporal = pl.pallas_call(
        functools.partial(plain_kernel, head_dim, share),
        out_shape=jax.ShapeDtypeStruct((rows, width), jnp.bfloat16),
        in_specs=[SMEM, VMEM, VMEM, VMEM],
        out_specs=VMEM,
        cost_estimate=cost(rows, width, 4),
        compiler_params=params(),
        name="temporalb",
    )(slopes, distance, gate_rows, moved)
    return lax.all_to_all(temporal, "frame", split_axis=0, concat_axis=0, tiled=True)


def permuted(arrays, slopes, distance, gate_rows, head_dim, share):
    (rows, width), count = arrays[0].shape, lax.axis_size("frame")
    held = [pltpu.with_memory_space_constraint(value, pltpu.HBM) for value in arrays]

    def gathered(some):
        return pl.pallas_call(
            functools.partial(gather_kernel, some, share, width),
            out_shape=[pltpu.VMEM((share, 3 * width), jnp.bfloat16) for _ in some],
            in_specs=[HBM] * 3,
            out_specs=[VMEM] * len(some),
            scratch_shapes=[pltpu.SemaphoreType.DMA((3 * len(some),))],
            compiler_params=params(),
            name="gather",
        )(*held)

    order = far_steps(count) + near_steps(count) + [0]
    blocks = dict(zip(order, [*gathered(order[:EARLY]), *gathered(order[EARLY:])]))
    landed = []
    for step in range(count):
        block = paired(blocks[step], step) if step else blocks[step]
        landed.append(pltpu.with_memory_space_constraint(block, pltpu.VMEM))
    temporal = pl.pallas_call(
        functools.partial(paired_kernel, count, head_dim, share),
        out_shape=jax.ShapeDtypeStruct((rows, width), jnp.bfloat16),
        in_specs=[SMEM, VMEM, VMEM] + [VMEM] * count,
        out_specs=HBM,
        scratch_shapes=[
            pltpu.VMEM((rows, 3 * width), jnp.bfloat16),
            pltpu.VMEM((rows, width), jnp.bfloat16),
            pltpu.SemaphoreType.DMA((count,)),
        ],
        cost_estimate=cost(rows, width, 4),
        compiler_params=params(),
        name="temporal",
    )(slopes, distance, gate_rows, *landed)
    return lax.all_to_all(temporal, "frame", split_axis=0, concat_axis=0, tiled=True)


def body(queries, key_rows, value_rows, slopes, noise_level, frame_times):
    frame_rows, model_width = queries.shape
    head_count = slopes.shape[0]
    head_dim = model_width // head_count
    count = lax.axis_size("frame")
    share = frame_rows // count
    signal_gate, noise_gate = noise_gates(noise_level)
    slopes = slopes.astype(jnp.float32)
    arrays = (queries, key_rows, value_rows)
    carried = spatial_part(*arrays, signal_gate, head_dim)
    paired_up = in_pairs(frame_rows, count)
    distance, gate_rows = tables(frame_times, noise_gate, paired_up, share, head_dim)
    spread = permuted if paired_up else exchanged
    temporal = spread(arrays, slopes, distance, gate_rows, head_dim, share)
    return (carried.astype(jnp.float32) + temporal.astype(jnp.float32)).astype(jnp.bfloat16)


def solution(mesh):
    return jax.shard_map(
        body,
        mesh=mesh,
        in_specs=(
            P(("groups", "frame"), None),
            P(("groups", "frame"), None),
            P(("groups", "frame"), None),
            P(),
            P("groups"),
            P("groups"),
        ),
        out_specs=P(("groups", "frame"), None),
        check_vma=False,
    )
```

```python
import functools
import math

import jax
import jax.numpy as jnp
from jax import lax
from jax.experimental import pallas as pl
from jax.experimental.pallas import tpu as pltpu
from jax.sharding import PartitionSpec as P


LEVELS = 1000
FAR = 1e30
VMEM_BYTES = 24 << 20
SUBLANES = 8
EARLY = 2
SPLIT = (9, 16)
LOG2_E = math.log2(math.e)
VMEM = pl.BlockSpec(memory_space=pltpu.VMEM)
SMEM = pl.BlockSpec(memory_space=pltpu.SMEM)
HBM = pl.BlockSpec(memory_space=pltpu.HBM)
ANY = pl.BlockSpec(memory_space=pl.ANY)


def shifted(value, axis, steps):
    count = lax.axis_size(axis)
    first, last = (max(0, -steps), min(count, count - steps))
    return lax.ppermute(value, axis, [(source, source + steps) for source in range(first, last)])


def paired(value, step):
    count = lax.axis_size("frame")
    return lax.ppermute(value, "frame", [(device, device ^ step) for device in range(count)])


def noise_gates(noise_level):
    phase = (noise_level.astype(jnp.float32) / LEVELS + 0.008) / 1.008
    cosine = jnp.cos(phase * (math.pi / 2))
    signal = cosine * cosine
    return (jnp.sqrt(signal), jnp.sqrt(1.0 - signal))


def in_pairs(frame_rows, count):
    return frame_rows % (SUBLANES * count) == 0 and count >= 4 and count & (count - 1) == 0


def far_steps(count):
    half, quarter = count // 2, count // 4
    return [half + offset + side for offset in range(quarter) for side in (quarter, 0)]


def near_steps(count):
    return list(range(count // 2 - 1, 0, -1))


def attend_heads(query_of, key_of, value_of, slope_of, distance, head_count, head_dim):
    factor = LOG2_E / math.sqrt(head_dim)
    heads = range(head_count)
    scores = [
        lax.dot_general(key_of(head), query_of(head), (((1,), (1,)), ((), ())), preferred_element_type=jnp.float32)
        * factor
        for head in heads
    ]
    if distance is not None:
        scores = [score - (slope_of(head) * LOG2_E) * distance for score, head in zip(scores, heads)]
    peaks = [jnp.max(score, axis=0, keepdims=True) for score in scores]
    raised = [jnp.exp2(score - peak) for score, peak in zip(scores, peaks)]
    shares = [1.0 / jnp.sum(value, axis=0, keepdims=True) for value in raised]
    weights = [(value * share).astype(jnp.bfloat16) for value, share in zip(raised, shares)]
    return [
        lax.dot_general(weight, value_of(head), (((0,), (0,)), ((), ())), preferred_element_type=jnp.float32)
        for weight, head in zip(weights, heads)
    ]


def run_copies(sem, pairs):
    copies = [pltpu.make_async_copy(source, target, sem.at[place]) for place, (source, target) in enumerate(pairs)]
    for copy in copies:
        copy.start()
    for copy in copies:
        copy.wait()


def rows_at(ref, block, share):
    return ref.at[pl.ds(pl.multiple_of(block * share, share), share), :]


def gather_kernel(turns, share, width, query_ref, key_ref, value_ref, *rest):
    outs, sem = rest[:-1], rest[-1]
    chip = lax.axis_index("frame") >> 1
    rows, pairs = 2 * share, []
    for place, turn in enumerate(turns):
        start = pl.multiple_of((chip ^ turn) * rows, rows)
        for part, source in enumerate((query_ref, key_ref, value_ref)):
            pairs.append(
                (source.at[pl.ds(start, rows), pl.ds(0, width)], outs[place].at[:, pl.ds(part * width, width)])
            )
    run_copies(sem, pairs)


def assembly(blocks, sibling_ref, out_ref, share):
    me = lax.axis_index("frame")
    core, chip = me & 1, me >> 1
    pairs = []
    for turn, block in enumerate(blocks):
        home = 2 * (chip ^ turn)
        pairs.append((rows_at(block, core, share), rows_at(out_ref, home + core, share)))
        pairs.append((sibling_ref.at[pl.ds(turn * share, share), :], rows_at(out_ref, home + 1 - core, share)))
    return pairs


def paired_kernel(turns, head_dim, share, slopes_ref, distance_ref, gate_ref, *rest):
    blocks, sibling_ref, outs = rest[:turns], rest[turns], rest[turns + 1 : 2 * turns + 1]
    moved_ref, result_ref, sem = rest[2 * turns + 1 :]
    run_copies(sem, assembly(blocks, sibling_ref, moved_ref, share))
    width, count = result_ref.shape[1], 2 * turns
    gate = gate_ref[...]
    part = lambda index: lambda head: moved_ref[:, pl.ds(index * width + head * head_dim, head_dim)]
    attended = attend_heads(
        part(0), part(1), part(2), lambda head: slopes_ref[head], distance_ref[...], width // head_dim, head_dim
    )
    for head, value in enumerate(attended):
        result_ref[:, pl.ds(head * head_dim, head_dim)] = (value * gate).astype(result_ref.dtype)
    chip = lax.axis_index("frame") >> 1
    pairs = []
    for turn in range(turns):
        for side in range(2):
            frame = lax.rem(2 * (chip ^ turn) + side + 1, count)
            pairs.append((rows_at(result_ref, frame, share), outs[turn].at[pl.ds(side * share, share), :]))
    run_copies(sem, pairs)


def plain_kernel(head_dim, share, slopes_ref, distance_ref, gate_ref, moved_ref, out_ref):
    rows, width = out_ref.shape
    gate = gate_ref[...]
    kept = lax.broadcasted_iota(jnp.int32, (rows, head_dim), 0) < rows - share
    part = lambda index: lambda head: moved_ref[:, pl.ds(index * width + head * head_dim, head_dim)]
    attended = attend_heads(
        part(0), part(1), part(2), lambda head: slopes_ref[head], distance_ref[...], width // head_dim, head_dim
    )
    for head, value in enumerate(attended):
        earlier = pltpu.roll(value * gate, rows - share, 0)
        out_ref[:, pl.ds(head * head_dim, head_dim)] = jnp.where(kept, earlier, 0.0).astype(out_ref.dtype)


def spatial_kernel(head_dim, gate_ref, query_ref, key_ref, value_ref, out_ref):
    width = out_ref.shape[1]
    gate = gate_ref[lax.axis_index("frame")]
    part = lambda ref: lambda head: ref[:, pl.ds(head * head_dim, head_dim)]
    attended = attend_heads(part(query_ref), part(key_ref), part(value_ref), None, None, width // head_dim, head_dim)
    for head, value in enumerate(attended):
        out_ref[:, pl.ds(head * head_dim, head_dim)] = (value * gate).astype(out_ref.dtype)


def sibling_kernel(share, *refs):
    blocks, out_ref, sem = refs[:-2], refs[-2], refs[-1]
    other = 1 - (lax.axis_index("frame") & 1)
    run_copies(
        sem, [(rows_at(block, other, share), out_ref.at[pl.ds(turn * share, share), :]) for turn, block in enumerate(blocks)]
    )


def assemble_kernel(share, *refs):
    run_copies(refs[-1], assembly(refs[:-3], refs[-3], refs[-2], share))


def cost(rows, width, operands):
    return pl.CostEstimate(
        flops=4 * rows * rows * width, bytes_accessed=operands * 2 * rows * width, transcendentals=rows * rows * 16
    )


def params():
    return pltpu.CompilerParams(vmem_limit_bytes=VMEM_BYTES)


def table_kernel(share, times_ref, gate_ref, distance_ref, rows_ref):
    rows, width = distance_ref.shape[0], rows_ref.shape[1]
    count = rows // share
    times = [times_ref[place].astype(jnp.float32) for place in range(count)]
    lane = lax.broadcasted_iota(jnp.int32, (share, rows), 1)
    row = lax.broadcasted_iota(jnp.int32, (share, rows), 0)
    lane_times = jnp.zeros((share, rows), jnp.float32)
    for place, time in enumerate(times):
        lane_times = jnp.where(lax.div(lane, share) == place, time, lane_times)
    same = lax.rem(lane, share) == row
    for place, time in enumerate(times):
        span = pl.ds(place * share, share)
        distance_ref[span, :] = jnp.where(same, jnp.abs(lane_times - time), FAR)
        gate = gate_ref[place] if place else 0.0
        rows_ref[span, :] = jnp.full((share, width), gate, jnp.float32)


def tables(frame_times, noise_gate, share, head_dim):
    rows = frame_times.shape[0] * share
    return pl.pallas_call(
        functools.partial(table_kernel, share),
        out_shape=[
            jax.ShapeDtypeStruct((rows, rows), jnp.float32),
            jax.ShapeDtypeStruct((rows, head_dim), jnp.float32),
        ],
        in_specs=[SMEM, SMEM],
        out_specs=[VMEM, VMEM],
        compiler_params=params(),
        name="tables",
    )(frame_times, noise_gate)


def spatial_part(queries, key_rows, value_rows, signal_gate, head_dim):
    frame_rows, model_width = queries.shape
    spatial = pl.pallas_call(
        functools.partial(spatial_kernel, head_dim),
        out_shape=jax.ShapeDtypeStruct((frame_rows, model_width), jnp.bfloat16),
        in_specs=[SMEM, VMEM, VMEM, VMEM],
        out_specs=VMEM,
        cost_estimate=cost(frame_rows, model_width, 4),
        compiler_params=params(),
        name="spatial",
    )(signal_gate, queries, key_rows, value_rows)
    return shifted(spatial, "frame", -1)


def exchanged(arrays, slopes, distance, gate_rows, head_dim, share):
    rows, width = arrays[0].shape
    moved = lax.all_to_all(jnp.concatenate(arrays, axis=1), "frame", split_axis=0, concat_axis=0, tiled=True)
    temporal = pl.pallas_call(
        functools.partial(plain_kernel, head_dim, share),
        out_shape=jax.ShapeDtypeStruct((rows, width), jnp.bfloat16),
        in_specs=[SMEM, VMEM, VMEM, VMEM],
        out_specs=VMEM,
        cost_estimate=cost(rows, width, 4),
        compiler_params=params(),
        name="temporalb",
    )(slopes, distance, gate_rows, moved)
    return lax.all_to_all(temporal, "frame", split_axis=0, concat_axis=0, tiled=True)


def turn_order(count):
    return [step // 2 for step in far_steps(count) + near_steps(count) if step % 2 == 0]


def across_chips(blocks, share):
    landed = []
    for turn, block in enumerate(blocks):
        landed.append(paired(block, 2 * turn) if turn else block)
    sibling = pl.pallas_call(
        functools.partial(sibling_kernel, share),
        out_shape=jax.ShapeDtypeStruct((len(blocks) * share, blocks[0].shape[1]), jnp.bfloat16),
        in_specs=[ANY] * len(blocks),
        out_specs=VMEM,
        scratch_shapes=[pltpu.SemaphoreType.DMA((len(blocks),))],
        compiler_params=params(),
        name="sibling",
    )(*landed)
    return [*landed, paired(sibling, 1)]


def permuted(arrays, slopes, distance, gate_rows, head_dim, share):
    rows, count = arrays[0].shape[0], lax.axis_size("frame")
    turns, width = count // 2, slopes.shape[0] * head_dim
    held = [pltpu.with_memory_space_constraint(value, pltpu.HBM) for value in arrays]

    def gathered(some):
        return pl.pallas_call(
            functools.partial(gather_kernel, some, share, width),
            out_shape=[pltpu.VMEM((2 * share, 3 * width), jnp.bfloat16) for _ in some],
            in_specs=[HBM] * 3,
            out_specs=[VMEM] * len(some),
            scratch_shapes=[pltpu.SemaphoreType.DMA((3 * len(some),))],
            compiler_params=params(),
            name="gather",
        )(*held)

    order = turn_order(count) + [0]
    blocks = dict(zip(order, [*gathered(order[:EARLY]), *gathered(order[EARLY:])]))
    landed = across_chips([blocks[turn] for turn in range(turns)], share)
    outs = pl.pallas_call(
        functools.partial(paired_kernel, turns, head_dim, share),
        out_shape=[jax.ShapeDtypeStruct((2 * share, width), jnp.bfloat16) for _ in range(turns)],
        in_specs=[SMEM, VMEM, VMEM] + [ANY] * (turns + 1),
        out_specs=[VMEM] * turns,
        scratch_shapes=[
            pltpu.VMEM((rows, 3 * width), jnp.bfloat16),
            pltpu.VMEM((rows, width), jnp.bfloat16),
            pltpu.SemaphoreType.DMA((count,)),
        ],
        cost_estimate=cost(rows, width, 4),
        compiler_params=params(),
        name="temporala",
    )(slopes, distance, gate_rows, *landed)
    back = across_chips(outs, share)
    return pl.pallas_call(
        functools.partial(assemble_kernel, share),
        out_shape=jax.ShapeDtypeStruct((rows, width), jnp.bfloat16),
        in_specs=[ANY] * (turns + 1),
        out_specs=VMEM,
        scratch_shapes=[pltpu.SemaphoreType.DMA((count,))],
        compiler_params=params(),
        name="assemble",
    )(*back)


def body(queries, key_rows, value_rows, slopes, noise_level, frame_times):
    frame_rows, model_width = queries.shape
    head_count = slopes.shape[0]
    head_dim = model_width // head_count
    count = lax.axis_size("frame")
    share = frame_rows // count
    signal_gate, noise_gate = noise_gates(noise_level)
    slopes = slopes.astype(jnp.float32)
    arrays = (queries, key_rows, value_rows)
    carried = spatial_part(*arrays, signal_gate, head_dim)
    distance, gate_rows = tables(frame_times, noise_gate, share, head_dim)
    if in_pairs(frame_rows, count):
        first = head_count * SPLIT[0] // SPLIT[1]
        part_a = permuted(arrays, slopes[:first], distance, gate_rows, head_dim, share)
        later = [value[:, first * head_dim :] for value in arrays]
        part_b = exchanged(later, slopes[first:], distance, gate_rows, head_dim, share)
        temporal = jnp.concatenate([part_a, part_b], axis=1)
    else:
        temporal = exchanged(arrays, slopes, distance, gate_rows, head_dim, share)
    return (carried.astype(jnp.float32) + temporal.astype(jnp.float32)).astype(jnp.bfloat16)


def solution(mesh):
    return jax.shard_map(
        body,
        mesh=mesh,
        in_specs=(
            P(("groups", "frame"), None),
            P(("groups", "frame"), None),
            P(("groups", "frame"), None),
            P(),
            P("groups"),
            P("groups"),
        ),
        out_specs=P(("groups", "frame"), None),
        check_vma=False,
    )
```
